32 devices in a mesh: groups: 2 (over x), space: 16 (over z, y, core).
Axes of the slice: x: 2, y: 2, z: 4, core: 2. Of those that a mesh axis runs over, the one named last changes fastest.
Arguments:
- signal: float32 [65536, 128], P(('groups', 'space')), parts along dimension 0, may hold values from -12 to 12
- space_tiles: float32 [512, 64, 384], P('space'), may hold values from -0.3125 to 0.3125
- tree_precision: float32 [256, 128], P('groups'), parts along dimension 0, may hold values from -0.5 to 0.5
- send_tiles: int32 [16, 4, 8], P('space'), may hold values from 0 to 31, as said below
- column_tiles: int32 [512, 6], P('space'), may hold values from 0 to 63, as said below
Outputs:
- product: float32 [65536, 128], P(('groups', 'space')), parts along dimension 0
- quad_form: float32 [2], P('groups'), parts along dimension 0
The draws below stay inside these ranges and needn't reach their ends.
There are 2 independent parts, one for each index of `groups`. The reference program is written for one: setup_inputs(seed, part) draws one part's arguments, and reference() takes and returns one part's arrays. A program takes and returns all parts, laid end to end along the dimension named above; an argument that names none is the same for every part. Nothing has to cross between parts.
Inputs may be any that keep to these rules, and one draw needn't show every extreme that they name: `send_tiles`: within one list the tile numbers are distinct; a partition lists tiles only towards neighbours that exist on the grid, from 1 to 8 of them, and some partition lists 8 tiles east and another south; slots past a list's length hold other tiles. `column_tiles`: entry 0 of every tile row is the row's own tile; entries below 32 are the partition's own tiles; an entry 32 + d * 8 + j names slot j of the list received from direction d, and only slots within that list's length.
All inputs are finite; a program needn't handle non-finite values.
Results may differ from the reference program's by a relative error of at most 0.00022.
Values sent between devices are 32-bit elements; how exact they have to be, the bound alone decides.
No kernel may reach another device: no remote copies, remote signals or barrier semaphores. Data moves between devices by JAX's collectives and lax.ppermute only.
A program may use at most 64 MiB of HBM per device.

```python
import math
import jax
import jax.numpy as jnp
from jax import lax

S = 128
TN = 64
TD = 32
K = 6
CAP = 8
NODES = 32768
NODE_TILES = 512
N_SPACE = 16


def layout_draw(key):
    wide = N_SPACE // 8
    device = jnp.arange(N_SPACE, dtype=jnp.int32)
    column = device % wide
    rowpos = device // wide
    exists = jnp.stack([column < wide - 1, column > 0, rowpos < 7, rowpos > 0], axis=1)
    counts = jax.random.randint(jax.random.fold_in(key, 11), (N_SPACE, 4), 1, CAP + 1)
    counts = counts.at[0, 0].set(CAP).at[wide, 3].set(CAP)
    counts = jnp.where(exists, counts, 0).astype(jnp.int32)
    scores = jax.random.randint(jax.random.fold_in(key, 12), (N_SPACE, 4, TD), 0, 1 << 20)
    scores = scores * TD + jnp.arange(TD, dtype=jnp.int32)
    order = jnp.argsort(scores, axis=-1)[..., :CAP].astype(jnp.int32)
    return (counts, order)


def draw_send_tiles(key, part):
    counts, order = layout_draw(key)
    return order


def draw_column_tiles(key, part):
    counts, order = layout_draw(key)
    wide = N_SPACE // 8
    device = jnp.arange(N_SPACE, dtype=jnp.int32)
    steps = jnp.array([1, -1, wide, -wide], dtype=jnp.int32)
    sender = (device[:, None] - steps[None, :]) % N_SPACE
    received = counts[sender, jnp.arange(4, dtype=jnp.int32)[None, :]]
    rowtile = jnp.arange(TD, dtype=jnp.int32)
    local_pick = jax.random.randint(jax.random.fold_in(key, 13), (N_SPACE, TD, 5), 0, TD).astype(jnp.int32)
    entries = [jnp.broadcast_to(rowtile[None, :], (N_SPACE, TD))]
    for direction in range(4):
        remote = rowtile[None, :] < received[:, direction][:, None]
        slot_index = TD + direction * CAP + rowtile[None, :]
        entries.append(jnp.where(remote, slot_index, local_pick[:, :, direction]))
    entries.append(local_pick[:, :, 4])
    return jnp.stack(entries, axis=2).reshape(N_SPACE * TD, K).astype(jnp.int32)


def draw_signal(key, part):
    rows = jnp.arange(NODES, dtype=jnp.float32)[:, None]
    rise = 3.0 ** (0.5 * rows / NODES)
    species = jnp.exp(jax.random.uniform(jax.random.fold_in(key, 21), (1, S), jnp.float32, 0.0, math.log(3.2)))
    base = jax.random.normal(jax.random.fold_in(key, 23), (NODES, S), jnp.float32)
    values = base * rise * species
    return jnp.clip(values, -12.0, 12.0).astype(jnp.float32)


def block_scale(own_key, shape, split, smallest, top_value):
    def one(position, shards_of):
        draws = jax.random.uniform(jax.random.fold_in(jax.random.fold_in(own_key, 6), position), (shards_of,), jnp.float32, smallest / len(split), top_value / len(split))
        return jnp.repeat(jnp.exp(draws), shape[position] // shards_of).reshape((-1,) + (1,) * (len(shape) - position - 1))

    gain = one(*split[0])
    for cut in split[1:]:
        gain = gain * one(*cut)
    return gain


def noise(stream_key, extent, width, bound, cuts=(), kind=jnp.bfloat16):
    values = width * jax.random.normal(stream_key, extent, jnp.float32)
    if cuts:
        values = values * block_scale(stream_key, extent, cuts, -0.22, 0.18)
    return jnp.clip(values, -bound, bound).astype(kind)


def setup_inputs(seed: int = 0, part: int = 0) -> dict:
    key_list = jax.random.split(jax.random.key(seed), 6)
    own_keys = jax.random.split(jax.random.fold_in(key_list[5], part), 6)
    return {
        "signal": draw_signal(jax.random.fold_in(jax.random.fold_in(key_list[5], part), 71), part),
        "space_tiles": noise(key_list[1], (NODE_TILES, TN, K * TN), (K * TN) ** -0.5, 0.3125, ((0, 16),), jnp.float32),
        "tree_precision": noise(own_keys[2], (S, S), S ** -0.5, 0.5, (), jnp.float32),
        "send_tiles": draw_send_tiles(jax.random.fold_in(key_list[5], 71), part),
        "column_tiles": draw_column_tiles(jax.random.fold_in(key_list[5], 71), part),
    }


def global_columns(send_tiles, column_tiles):
    wide = N_SPACE // 8
    steps = jnp.array([1, -1, wide, -wide], dtype=jnp.int32)
    owner = (jnp.arange(NODE_TILES, dtype=jnp.int32) // TD)[:, None]
    local_part = jnp.minimum(column_tiles, TD - 1)
    remote = jnp.maximum(column_tiles - TD, 0)
    direction = remote // CAP
    slot = remote % CAP
    sender = (owner - steps[direction]) % N_SPACE
    listed = send_tiles[sender, direction, slot]
    return jnp.where(column_tiles < TD, owner * TD + local_part, sender * TD + listed).astype(jnp.int32)

def reference(signal, space_tiles, tree_precision, send_tiles, column_tiles):
    columns = global_columns(send_tiles, column_tiles)
    tiled = signal.reshape(NODE_TILES, TN, S)
    col_blocks = columns.reshape(N_SPACE, TD, K)
    tile_blocks = space_tiles.reshape(N_SPACE, TD, TN, K * TN)

    def one_part(pair):
        cols, tiles = pair
        gathered = tiled[cols].reshape(TD, K * TN, S)
        return jnp.einsum('rac,rcs->ras', tiles, gathered, precision=lax.Precision.HIGHEST)
    spatial = lax.map(one_part, (col_blocks, tile_blocks)).reshape(NODES, S)
    product = jnp.dot(spatial, tree_precision.T, precision=lax.Precision.HIGHEST, preferred_element_type=jnp.float32)
    quad_form = jnp.sum(signal * product) / jnp.sqrt(jnp.float32(NODES * S))
    return (product, quad_form.reshape(1))
```

```python
import math

import jax
import jax.numpy as jnp
from jax import lax
from jax.experimental import pallas as pl
from jax.experimental.pallas import tpu as pltpu
from jax.sharding import PartitionSpec as P

ROWS = 8
ANY = pl.BlockSpec(memory_space=pl.ANY)
SMEM = pl.BlockSpec(memory_space=pltpu.SMEM)
VMEM = pl.BlockSpec(memory_space=pltpu.VMEM)
PARAMS = pltpu.CompilerParams(vmem_limit_bytes=40 * 1024 * 1024)


def split(x):
    high = x.astype(jnp.bfloat16)
    return high, (x - high.astype(jnp.float32)).astype(jnp.bfloat16)


def stacked(x):
    return jnp.concatenate(split(x), axis=0)


def side_by_side(x):
    return jnp.concatenate(split(x), axis=1)


def dot(a, b, dims):
    return lax.dot_general(a, b, (dims, ((), ())), preferred_element_type=jnp.float32)


def quarters(s):
    rows, lanes = s.shape[0] // 2, s.shape[1] // 2
    return (s[rows:, lanes:] + s[rows:, :lanes]) + s[:rows, lanes:] + s[:rows, :lanes]


def slot_of(column, own, cap, merged):
    entry = column - own
    if merged:
        return jnp.where(entry < 2 * cap, entry % cap, entry - cap)
    return entry


def pick(lists, tiled, wide, merged):
    cap = lists.shape[2]
    count = 3 if merged else 4
    shape = jax.ShapeDtypeStruct((cap,) + tiled.shape[1:], tiled.dtype)

    def kernel(lists_ref, tiled_ref, *rest):
        outs, sems = rest[:count], rest[count]
        if merged:
            column = lax.axis_index("space") % wide
            directions = [jnp.where(column == 0, 0, 1), 2, 3]
        else:
            directions = [0, 1, 2, 3]
        copies = []
        for i in (2, 1, 0) if merged else range(count):
            for j in range(cap):
                tile = lists_ref[0, directions[i], j]
                copies.append(pltpu.make_async_copy(tiled_ref.at[tile], outs[i].at[j], sems.at[i, j]))
                copies[-1].start()
        for copy in copies:
            copy.wait()

    return pl.pallas_call(
        kernel,
        out_shape=[shape] * count,
        in_specs=[SMEM, ANY],
        out_specs=[ANY] * count,
        scratch_shapes=[pltpu.SemaphoreType.DMA((count, cap))],
        name="pick",
    )(lists, tiled)


def exchange(outgoing, wide, merged):
    count = lax.axis_size("space")
    if merged:
        routes = [[(i, i ^ 1) for i in range(count)]]
    else:
        routes = [
            [(i - 1, i) for i in range(count) if i % wide > 0],
            [(i + 1, i) for i in range(count) if i % wide < wide - 1],
        ]
    routes.append([(i - wide, i) for i in range(wide, count)])
    routes.append([(i + wide, i) for i in range(count - wide)])
    return [lax.ppermute(o, "space", r) for o, r in zip(outgoing, routes)]


def local_part(columns, tiled, space_tiles, tree, slots, cap, merged):
    own, nodes, species = tiled.shape
    stored = columns.shape[0]
    wide_k = stored * nodes
    chunk = 4

    def kernel(columns_ref, x_ref, a_ref, tree_ref, product_ref, v_ref, quad_ref, xs_ref, z_ref, sp_ref):
        for c in range(0, own, chunk):
            x = x_ref[c : c + chunk].reshape(chunk * nodes, species)
            xs_ref[c : c + chunk] = side_by_side(x).reshape(chunk, nodes, 2 * species)
        xs_ref[own] = jnp.zeros((nodes, 2 * species), jnp.bfloat16)
        v_ref[...] = jnp.zeros(v_ref.shape, jnp.float32)
        tree_rows = stacked(tree_ref[...])
        tree_lanes = side_by_side(tree_ref[...])

        def row(t, _):
            tiles = []
            for k in range(stored):
                column = columns_ref[k, t]
                tiles.append(xs_ref[jnp.where(column < own, column, own)])
            gathered = jnp.concatenate(tiles, axis=0)
            sp_ref[t] = quarters(dot(stacked(a_ref[t]), gathered, ((1,), (0,))))
            return 0

        lax.fori_loop(0, own, row, 0, unroll=2)

        quad = jnp.zeros((8, species), jnp.float32)
        for c in range(0, own, chunk):
            xs = xs_ref[c : c + chunk].reshape(chunk * nodes, 2 * species)
            x = jnp.concatenate([xs[:, :species], xs[:, species:]], axis=0)
            z = quarters(dot(x, tree_lanes, ((1,), (0,))))
            z_ref[c : c + chunk] = z.reshape(chunk, nodes, species)
            spatial = sp_ref[c : c + chunk].reshape(chunk * nodes, species)
            product = quarters(dot(stacked(spatial), tree_rows, ((1,), (1,))))
            product_ref[c : c + chunk] = product.reshape(chunk, nodes, species)
            quad = quad + (z * spatial).reshape(-1, 8, species).sum(axis=0)
        quad_ref[...] = quad

        def remote_row(t, _):
            columns = [columns_ref[k, t] for k in range(stored)]
            last = columns[0]
            for column in columns[1:]:
                last = jnp.maximum(last, column)

            @pl.when(last >= own)
            def _():
                z = side_by_side(z_ref[t])
                w = dot(stacked(a_ref[t]), jnp.concatenate([z, z], axis=0), ((0,), (0,)))
                w = w[:, species:] + w[:, :species]
                for k in range(stored):

                    @pl.when(columns[k] >= own)
                    def _():
                        slot = slot_of(columns[k], own, cap, merged)
                        v_ref[slot] += w[k * nodes : (k + 1) * nodes]

            return 0

        lax.fori_loop(0, own, remote_row, 0)

    return pl.pallas_call(
        kernel,
        out_shape=[
            jax.ShapeDtypeStruct(tiled.shape, jnp.float32),
            jax.ShapeDtypeStruct((slots, nodes, species), jnp.float32),
            jax.ShapeDtypeStruct((8, species), jnp.float32),
        ],
        in_specs=[SMEM, VMEM, VMEM, VMEM],
        out_specs=[VMEM, VMEM, VMEM],
        scratch_shapes=[
            pltpu.VMEM((own + 1, nodes, 2 * species), jnp.bfloat16),
            pltpu.VMEM(tiled.shape, jnp.float32),
            pltpu.VMEM(tiled.shape, jnp.float32),
        ],
        compiler_params=PARAMS,
        name="local_part",
    )(columns, tiled, space_tiles, tree)


def remote_quad(v, received, quad, count):
    species = v.shape[2]
    cap = received[0].shape[0]

    def kernel(v_ref, quad_ref, *rest):
        parts, out_ref = rest[:-1], rest[-1]
        total = quad_ref[...]
        for i, part in enumerate(parts):
            for j in range(cap):
                total = total + (v_ref[i * cap + j] * part[j]).reshape(-1, 8, species).sum(axis=0)
        total = total.sum(axis=0, keepdims=True)
        for i in range(count):
            out_ref[i] = total

    return pl.pallas_call(
        kernel,
        out_shape=jax.ShapeDtypeStruct((count, 1, species), jnp.float32),
        in_specs=[VMEM] * (2 + len(received)),
        out_specs=VMEM,
        compiler_params=PARAMS,
        name="remote_quad",
    )(v, quad, *received)


def remote_part(columns, space_tiles, tree, product, received, sums, scale, merged):
    own, nodes, species = product.shape
    stored = columns.shape[0]
    cap = received[0].shape[0]
    slots = len(received) * cap
    groups = len(received)

    def kernel(columns_ref, tree_ref, sums_ref, a_hbm, product_hbm, *rest):
        parts = rest[:groups]
        out_hbm, quad_ref, x_ref, xs_ref, a_ref, p_ref, x_sem, a_sem, p_sem, o_sem = rest[groups:]
        copies = [pltpu.make_async_copy(parts[i], x_ref.at[pl.ds(i * cap, cap)], x_sem.at[i]) for i in range(groups)]
        for copy in copies:
            copy.start()

        def load_a(t):
            return pltpu.make_async_copy(a_hbm.at[t], a_ref.at[t], a_sem.at[t])

        def load_p(t):
            return pltpu.make_async_copy(product_hbm.at[t], p_ref.at[t], p_sem.at[t])

        def store_p(t):
            return pltpu.make_async_copy(p_ref.at[t], out_hbm.at[t], o_sem.at[t])

        def last_column(t):
            last = columns_ref[0, t]
            for k in range(1, stored):
                last = jnp.maximum(last, columns_ref[k, t])
            return last

        def each_remote(step):
            def body(t, _):
                @pl.when(last_column(t) >= own)
                def _():
                    step(t)

                return 0

            lax.fori_loop(0, own, body, 0)

        def fetch(t):
            load_a(t).start()
            load_p(t).start()

        each_remote(fetch)
        quad_ref[0] = jnp.sum(sums_ref[...]) * scale
        tree_rows = stacked(tree_ref[...])
        xs_ref[slots] = jnp.zeros((nodes, 2 * species), jnp.bfloat16)
        for i, copy in enumerate(copies):
            copy.wait()
            x = x_ref[i * cap : (i + 1) * cap].reshape(cap * nodes, species)
            xs_ref[i * cap : (i + 1) * cap] = side_by_side(x).reshape(cap, nodes, 2 * species)

        def work(t):
            tiles = []
            for k in range(stored):
                column = columns_ref[k, t]
                slot = slot_of(column, own, cap, merged)
                tiles.append(xs_ref[jnp.where(column < own, slots, slot)])
            load_a(t).wait()
            load_p(t).wait()
            spatial = quarters(dot(stacked(a_ref[t]), jnp.concatenate(tiles, axis=0), ((1,), (0,))))
            p_ref[t] += quarters(dot(stacked(spatial), tree_rows, ((1,), (1,))))
            store_p(t).start()

        each_remote(work)
        each_remote(lambda t: store_p(t).wait())

    return pl.pallas_call(
        kernel,
        out_shape=[jax.ShapeDtypeStruct(product.shape, jnp.float32), jax.ShapeDtypeStruct((1,), jnp.float32)],
        in_specs=[SMEM, VMEM, VMEM, ANY, ANY] + [ANY] * groups,
        out_specs=[ANY, SMEM],
        scratch_shapes=[
            pltpu.VMEM((slots, nodes, species), jnp.float32),
            pltpu.VMEM((slots + 1, nodes, 2 * species), jnp.bfloat16),
            pltpu.VMEM(space_tiles.shape, jnp.float32),
            pltpu.VMEM(product.shape, jnp.float32),
            pltpu.SemaphoreType.DMA((groups,)),
            pltpu.SemaphoreType.DMA((own,)),
            pltpu.SemaphoreType.DMA((own,)),
            pltpu.SemaphoreType.DMA((own,)),
        ],
        input_output_aliases={4: 0},
        compiler_params=PARAMS,
        name="remote_part",
    )(columns, tree, sums, space_tiles, product, *received)


def on_device(signal, space_tiles, tree_precision, send_tiles, column_tiles):
    count = lax.axis_size("space")
    wide = count // ROWS
    merged = wide == 2
    tile_rows, tile_nodes = space_tiles.shape[:2]
    species = signal.shape[1]
    cap = send_tiles.shape[2]
    tiled = signal.reshape(tile_rows, tile_nodes, species)
    columns = column_tiles.T
    outgoing = pick(send_tiles, tiled, wide, merged)
    received = exchange(outgoing, wide, merged)
    slots = len(received) * cap
    product, v, quad = local_part(columns, tiled, space_tiles, tree_precision, slots, cap, merged)
    shares = remote_quad(v, received, quad, count)
    sums = lax.all_to_all(shares, "space", 0, 0)
    scale = 1.0 / math.sqrt(count * tile_rows * tile_nodes * species)
    product, total = remote_part(columns, space_tiles, tree_precision, product, received, sums, scale, merged)
    return product.reshape(signal.shape), total


def solution(mesh):
    placed = (
        P(("groups", "space"), None),
        P("space", None, None),
        P("groups", None),
        P("space", None, None),
        P("space", None),
    )
    return jax.shard_map(
        on_device,
        mesh=mesh,
        in_specs=placed,
        out_specs=(P(("groups", "space"), None), P("groups")),
        check_vma=False,
    )
```

```python
import math

import jax
import jax.numpy as jnp
from jax import lax
from jax.experimental import pallas as pl
from jax.experimental.pallas import tpu as pltpu
from jax.sharding import PartitionSpec as P

ROWS = 8
BLOCK = 4
HBM = pl.BlockSpec(memory_space=pltpu.HBM)
SMEM = pl.BlockSpec(memory_space=pltpu.SMEM)
VMEM = pl.BlockSpec(memory_space=pltpu.VMEM)
MIB = 1024 * 1024


def in_hbm(x):
    return pltpu.with_memory_space_constraint(x, pltpu.HBM)


def split(x):
    high = x.astype(jnp.bfloat16)
    return high, (x - high.astype(jnp.float32)).astype(jnp.bfloat16)


def stacked(x):
    return jnp.concatenate(split(x), axis=0)


def side_by_side(x):
    return jnp.concatenate(split(x), axis=1)


def dot(a, b, dims):
    return lax.dot_general(a, b, (dims, ((), ())), preferred_element_type=jnp.float32)


def quarters(s):
    rows, lanes = s.shape[0] // 2, s.shape[1] // 2
    return (s[rows:, lanes:] + s[rows:, :lanes]) + s[:rows, lanes:] + s[:rows, :lanes]


class Exchange:
    def __init__(self, count, cap):
        self.count, self.cap = count, cap
        self.wide = count // ROWS
        self.legs = [(self.wide, 0, 2, 3)]
        if ROWS > 2:
            self.legs.append((self.wide, 1, 2, 3))
        if self.wide > 1:
            self.legs.append((1, 0, 0, 1))
        if self.wide > 2:
            self.legs.append((1, 1, 0, 1))
        self.slots = len(self.legs) * cap

    def place(self, device, step):
        return device // self.wide if step == self.wide else device % self.wide

    def extent(self, step):
        return ROWS if step == self.wide else self.wide

    def route(self, leg):
        step, odd = leg[:2]
        pairs = []
        for i in range(self.count):
            at = self.place(i, step)
            if at % 2 == odd and at + 1 < self.extent(step):
                pairs += [(i, i + step), (i + step, i)]
        return pairs

    def sends(self, leg, device):
        step, odd, up, down = leg
        return jnp.where(self.place(device, step) % 2 == odd, up, down)

    def slot(self, column, own, device):
        entry = column - own
        direction = entry // self.cap
        base = jnp.int32(0)
        for i, leg in enumerate(self.legs):
            base = jnp.where(direction == leg[2] + leg[3] - self.sends(leg, device), i * self.cap, base)
        return jnp.where(entry < 0, self.slots, base + entry % self.cap)


def pick(lists, tiled, plan):
    cap, legs = plan.cap, plan.legs
    shape = pltpu.VMEM((cap,) + tiled.shape[1:], tiled.dtype)

    def kernel(lists_ref, tiled_ref, *rest):
        outs = rest[: len(legs)]
        numbers, sems, sem = rest[len(legs) :]
        device = lax.axis_index("space")
        load = pltpu.make_async_copy(lists_ref, numbers, sem)
        load.start()
        load.wait()
        copies = []
        for i, leg in enumerate(legs):
            direction = plan.sends(leg, device)
            for j in range(cap):
                tile = numbers[0, direction, j]
                copies.append(pltpu.make_async_copy(tiled_ref.at[tile], outs[i].at[j], sems.at[i, j]))
                copies[-1].start()
        for copy in copies:
            copy.wait()

    return pl.pallas_call(
        kernel,
        out_shape=[shape] * len(legs),
        in_specs=[HBM, HBM],
        out_specs=[VMEM] * len(legs),
        scratch_shapes=[
            pltpu.SMEM(lists.shape, jnp.int32),
            pltpu.SemaphoreType.DMA((len(legs), cap)),
            pltpu.SemaphoreType.DMA(()),
        ],
        compiler_params=pltpu.CompilerParams(vmem_limit_bytes=4 * MIB),
        name="pick",
    )(in_hbm(lists), in_hbm(tiled))


def local_part(columns, tiled, space_tiles, tree, plan):
    own, nodes, species = tiled.shape
    stored = columns.shape[0]
    slots = plan.slots
    block = BLOCK * nodes

    def kernel(columns_hbm, x_hbm, a_hbm, tree_hbm, product_hbm, p_ref, v_ref, quad_ref, meta_ref, *scratch):
        columns_ref, x_ref, a_ref, tree_ref, xs_ref, z_ref, c_sem, x_sem, a_sem, t_sem, sem = scratch
        device = lax.axis_index("space")

        def load(hbm, ref, sems, b):
            at = pl.ds(b * BLOCK, BLOCK)
            return pltpu.make_async_copy(hbm.at[at], ref.at[at], sems.at[b])

        load_columns = pltpu.make_async_copy(columns_hbm, columns_ref, c_sem)
        load_tree = pltpu.make_async_copy(tree_hbm, tree_ref, t_sem)
        for b in range(own // BLOCK):
            load(x_hbm, x_ref, x_sem, b).start()
        load_columns.start()
        load_tree.start()
        for b in range(own // BLOCK):
            load(a_hbm, a_ref, a_sem, b).start()
        xs_ref[own] = jnp.zeros((nodes, 2 * species), jnp.bfloat16)
        v_ref[...] = jnp.zeros(v_ref.shape, jnp.float32)
        for b in range(own // BLOCK):
            load(x_hbm, x_ref, x_sem, b).wait()
            c = b * BLOCK
            x = x_ref[c : c + BLOCK].reshape(block, species)
            xs_ref[c : c + BLOCK] = side_by_side(x).reshape(BLOCK, nodes, 2 * species)
        load_columns.wait()
        load_tree.wait()
        tree_rows = stacked(tree_ref[...])
        tree_lanes = side_by_side(tree_ref[...])

        def store(b):
            at = pl.ds(b * BLOCK, BLOCK)
            return pltpu.make_async_copy(p_ref.at[at], product_hbm.at[at], sem.at[b])

        def rows(b, carry):
            remote, quad = carry
            load(a_hbm, a_ref, a_sem, b).wait()
            parts = []
            for u in range(BLOCK):
                t = b * BLOCK + u
                tiles, last = [], jnp.int32(0)
                meta_ref[0, remote] = t
                for k in range(stored):
                    column = columns_ref[k, t]
                    last = jnp.maximum(last, column)
                    meta_ref[1 + k, remote] = plan.slot(column, own, device)
                    tiles.append(xs_ref[jnp.minimum(column, own)])
                remote = remote + (last >= own).astype(jnp.int32)
                parts.append(quarters(dot(stacked(a_ref[t]), jnp.concatenate(tiles, axis=0), ((1,), (0,)))))
            spatial = jnp.concatenate(parts, axis=0)
            at = pl.ds(b * BLOCK, BLOCK)
            xs = xs_ref[at].reshape(block, 2 * species)
            x = jnp.concatenate([xs[:, :species], xs[:, species:]], axis=0)
            z = quarters(dot(x, tree_lanes, ((1,), (0,))))
            z_ref[at] = z.reshape(BLOCK, nodes, species)
            product = quarters(dot(stacked(spatial), tree_rows, ((1,), (1,))))
            p_ref[at] = product.reshape(BLOCK, nodes, species)
            store(b).start()
            return remote, quad + (z * spatial).reshape(-1, 8, species).sum(axis=0)

        remote, quad = lax.fori_loop(0, own // BLOCK, rows, (jnp.int32(0), jnp.zeros((8, species), jnp.float32)))
        quad_ref[...] = quad
        blocks = (remote + BLOCK - 1) // BLOCK
        last_row = meta_ref[0, jnp.maximum(remote - 1, 0)]
        for u in range(BLOCK):
            meta_ref[0, remote + u] = last_row
            for k in range(stored):
                meta_ref[1 + k, remote + u] = slots
        meta_ref[1 + stored, 0] = remote

        def remote_rows(b, _):
            for u in range(BLOCK):
                i = b * BLOCK + u
                t = meta_ref[0, i]
                z = side_by_side(z_ref[t])
                w = dot(stacked(a_ref[t]), jnp.concatenate([z, z], axis=0), ((0,), (0,)))
                w = w[:, species:] + w[:, :species]
                for k in range(stored):
                    v_ref[meta_ref[1 + k, i]] += w[k * nodes : (k + 1) * nodes]
            return 0

        lax.fori_loop(0, blocks, remote_rows, 0)
        for b in range(own // BLOCK):
            store(b).wait()

    return pl.pallas_call(
        kernel,
        out_shape=[
            pltpu.HBM(tiled.shape, jnp.float32),
            pltpu.VMEM(tiled.shape, jnp.float32),
            pltpu.VMEM((slots + 1, nodes, species), jnp.float32),
            pltpu.VMEM((8, species), jnp.float32),
            pltpu.SMEM((stored + 2, own + BLOCK), jnp.int32),
        ],
        in_specs=[HBM] * 4,
        out_specs=[HBM, VMEM, VMEM, VMEM, SMEM],
        scratch_shapes=[
            pltpu.SMEM(columns.shape, jnp.int32),
            pltpu.VMEM(tiled.shape, jnp.float32),
            pltpu.VMEM(space_tiles.shape, jnp.float32),
            pltpu.VMEM(tree.shape, jnp.float32),
            pltpu.VMEM((own + 1, nodes, 2 * species), jnp.bfloat16),
            pltpu.VMEM(tiled.shape, jnp.float32),
            pltpu.SemaphoreType.DMA(()),
            pltpu.SemaphoreType.DMA((own // BLOCK,)),
            pltpu.SemaphoreType.DMA((own // BLOCK,)),
            pltpu.SemaphoreType.DMA(()),
            pltpu.SemaphoreType.DMA((own // BLOCK,)),
        ],
        compiler_params=pltpu.CompilerParams(vmem_limit_bytes=16 * MIB),
        name="local_part",
    )(in_hbm(columns), in_hbm(tiled), in_hbm(space_tiles), in_hbm(tree))


def remote_quad(v, quad, received, count):
    species = v.shape[2]
    cap = received[0].shape[0]

    def kernel(v_ref, quad_ref, *rest):
        parts, out_ref = rest[:-1], rest[-1]
        total = quad_ref[...]
        for i, part in enumerate(parts):
            for j in range(cap):
                total = total + (v_ref[i * cap + j] * part[j]).reshape(-1, 8, species).sum(axis=0)
        total = total.sum(axis=0, keepdims=True)
        for i in range(count):
            out_ref[i] = total

    return pl.pallas_call(
        kernel,
        out_shape=jax.ShapeDtypeStruct((count, 1, species), jnp.float32),
        in_specs=[VMEM] * (2 + len(received)),
        out_specs=VMEM,
        compiler_params=pltpu.CompilerParams(vmem_limit_bytes=8 * MIB),
        name="remote_quad",
    )(v, quad, *received)


def remote_part(meta, space_tiles, tree, local, product, received):
    own, nodes, species = product.shape
    stored = meta.shape[0] - 2
    legs, cap = len(received), received[0].shape[0]
    slots = legs * cap

    def kernel(meta_ref, tree_hbm, a_hbm, p_ref, *rest):
        parts = rest[:legs]
        _, out_hbm, tree_ref, a_ref, xs_ref, o_ref, t_sem, a_sem, sem = rest[legs:]
        remote = meta_ref[1 + stored, 0]
        padded = (remote + BLOCK - 1) // BLOCK * BLOCK

        def load(i):
            return pltpu.make_async_copy(a_hbm.at[meta_ref[0, i]], a_ref.at[i], a_sem.at[i])

        def begin(i, _):
            load(i).start()
            return 0

        load_tree = pltpu.make_async_copy(tree_hbm, tree_ref, t_sem)
        load_tree.start()
        lax.fori_loop(0, padded, begin, 0)
        xs_ref[slots] = jnp.zeros((nodes, 2 * species), jnp.bfloat16)
        for i in range(legs):
            x = parts[i][...].reshape(cap * nodes, species)
            xs_ref[i * cap : (i + 1) * cap] = side_by_side(x).reshape(cap, nodes, 2 * species)
        load_tree.wait()
        tree_rows = stacked(tree_ref[...])

        def store(i):
            return pltpu.make_async_copy(o_ref.at[i], out_hbm.at[meta_ref[0, i]], sem.at[i])

        def work(b, _):
            sums = []
            for u in range(BLOCK):
                i = b * BLOCK + u
                tiles = [xs_ref[meta_ref[1 + k, i]] for k in range(stored)]
                load(i).wait()
                a = stacked(a_ref[i])
                sums.append(quarters(dot(a, jnp.concatenate(tiles, axis=0), ((1,), (0,)))))
            added = quarters(dot(stacked(jnp.concatenate(sums, axis=0)), tree_rows, ((1,), (1,))))
            for u in range(BLOCK):
                i = b * BLOCK + u
                o_ref[i] = p_ref[meta_ref[0, i]] + added[u * nodes : (u + 1) * nodes]

                @pl.when(i < remote)
                def _():
                    store(i).start()

            return 0

        lax.fori_loop(0, padded // BLOCK, work, 0)

        def finish(i, _):
            store(i).wait()
            return 0

        lax.fori_loop(0, remote, finish, 0)

    return pl.pallas_call(
        kernel,
        out_shape=pltpu.HBM(product.shape, jnp.float32),
        in_specs=[SMEM, HBM, HBM] + [VMEM] * (1 + legs) + [HBM],
        out_specs=HBM,
        scratch_shapes=[
            pltpu.VMEM(tree.shape, jnp.float32),
            pltpu.VMEM((own + BLOCK,) + space_tiles.shape[1:], jnp.float32),
            pltpu.VMEM((slots + 1, nodes, 2 * species), jnp.bfloat16),
            pltpu.VMEM((own + BLOCK, nodes, species), jnp.float32),
            pltpu.SemaphoreType.DMA(()),
            pltpu.SemaphoreType.DMA((own + BLOCK,)),
            pltpu.SemaphoreType.DMA((own,)),
        ],
        input_output_aliases={4 + legs: 0},
        compiler_params=pltpu.CompilerParams(vmem_limit_bytes=16 * MIB),
        name="remote_part",
    )(meta, in_hbm(tree), in_hbm(space_tiles), local, *received, in_hbm(product))


def on_device(signal, space_tiles, tree_precision, send_tiles, column_tiles):
    count = lax.axis_size("space")
    tile_rows, tile_nodes = space_tiles.shape[:2]
    species = signal.shape[1]
    plan = Exchange(count, send_tiles.shape[2])
    tiled = signal.reshape(tile_rows, tile_nodes, species)
    outgoing = pick(send_tiles, tiled, plan)
    received = [lax.ppermute(o, "space", plan.route(leg)) for o, leg in zip(outgoing, plan.legs)]
    product, local, v, quad, meta = local_part(column_tiles.T, tiled, space_tiles, tree_precision, plan)
    shares = remote_quad(v, quad, received, count)
    sums = lax.all_to_all(shares, "space", 0, 0)
    product = remote_part(meta, space_tiles, tree_precision, local, product, received)
    scale = 1.0 / math.sqrt(count * tile_rows * tile_nodes * species)
    return product.reshape(signal.shape), (jnp.sum(sums) * scale).reshape(1)


def solution(mesh):
    placed = (
        P(("groups", "space"), None),
        P("space", None, None),
        P("groups", None),
        P("space", None, None),
        P("space", None),
    )
    return jax.shard_map(
        on_device,
        mesh=mesh,
        in_specs=placed,
        out_specs=(P(("groups", "space"), None), P("groups")),
        check_vma=False,
    )
```

```python
import math

import jax
import jax.numpy as jnp
from jax import lax
from jax.experimental import pallas as pl
from jax.experimental.pallas import tpu as pltpu
from jax.sharding import PartitionSpec as P

ROWS = 8
LOCAL_BLOCK = 8
BLOCK = 4
HBM = pl.BlockSpec(memory_space=pltpu.HBM)
SMEM = pl.BlockSpec(memory_space=pltpu.SMEM)
VMEM = pl.BlockSpec(memory_space=pltpu.VMEM)
MIB = 1024 * 1024


def in_hbm(x):
    return pltpu.with_memory_space_constraint(x, pltpu.HBM)


def split(x):
    high = x.astype(jnp.bfloat16)
    return high, (x - high.astype(jnp.float32)).astype(jnp.bfloat16)


def stacked(x):
    return jnp.concatenate(split(x), axis=0)


def side_by_side(x):
    return jnp.concatenate(split(x), axis=1)


def dot(a, b, dims):
    return lax.dot_general(a, b, (dims, ((), ())), preferred_element_type=jnp.float32)


def quarters(s):
    rows, lanes = s.shape[0] // 2, s.shape[1] // 2
    return (s[rows:, lanes:] + s[rows:, :lanes]) + s[:rows, lanes:] + s[:rows, :lanes]


def halves(s):
    lanes = s.shape[1] // 2
    return s[:, lanes:] + s[:, :lanes]


def tree_forward(tree):
    rows = stacked(tree)
    return jnp.concatenate([rows, rows], axis=1)


def tree_backward(tree):
    lanes = side_by_side(tree)
    return jnp.concatenate([lanes, lanes], axis=0)


class Exchange:
    def __init__(self, count, cap):
        self.count, self.cap = count, cap
        self.wide = count // ROWS
        self.legs = [(self.wide, 0, 2, 3)]
        if ROWS > 2:
            self.legs.append((self.wide, 1, 2, 3))
        if self.wide > 1:
            self.legs.append((1, 0, 0, 1))
        if self.wide > 2:
            self.legs.append((1, 1, 0, 1))
        self.slots = len(self.legs) * cap

    def place(self, device, step):
        return device // self.wide if step == self.wide else device % self.wide

    def extent(self, step):
        return ROWS if step == self.wide else self.wide

    def route(self, leg):
        step, odd = leg[:2]
        pairs = []
        for i in range(self.count):
            at = self.place(i, step)
            if at % 2 == odd and at + 1 < self.extent(step):
                pairs += [(i, i + step), (i + step, i)]
        return pairs

    def sends(self, leg, device):
        step, odd, up, down = leg
        return jnp.where(self.place(device, step) % 2 == odd, up, down)

    def slot(self, column, own, device):
        entry = column - own
        direction = entry // self.cap
        base = jnp.int32(0)
        for i, leg in enumerate(self.legs):
            base = jnp.where(direction == leg[2] + leg[3] - self.sends(leg, device), i * self.cap, base)
        return jnp.where(entry < 0, self.slots, base + entry % self.cap)


def pick(lists, tiled, plan):
    cap, legs = plan.cap, plan.legs
    chunks = 4
    chunk = tiled.shape[0] // chunks
    shape = pltpu.VMEM((cap,) + tiled.shape[1:], tiled.dtype)

    def kernel(lists_hbm, tiled_hbm, *rest):
        outs, tiled_ref = rest[: len(legs)], rest[len(legs)]
        lists_ref, sems, sem = rest[len(legs) + 1 :]
        loads = [pltpu.make_async_copy(lists_hbm, lists_ref, sem)]
        for i in range(chunks):
            at = pl.ds(i * chunk, chunk)
            loads.append(pltpu.make_async_copy(tiled_hbm.at[at], tiled_ref.at[at], sems.at[i]))
        for load in loads:
            load.start()
        device = lax.axis_index("space")
        directions = [plan.sends(leg, device) for leg in legs]
        for load in loads:
            load.wait()
        for i, direction in enumerate(directions):
            for j in range(cap):
                outs[i][j] = tiled_ref[lists_ref[0, direction, j]]

    return pl.pallas_call(
        kernel,
        out_shape=[shape] * len(legs) + [pltpu.VMEM(tiled.shape, tiled.dtype)],
        in_specs=[HBM, HBM],
        out_specs=[VMEM] * (len(legs) + 1),
        scratch_shapes=[
            pltpu.SMEM(lists.shape, jnp.int32),
            pltpu.SemaphoreType.DMA((chunks,)),
            pltpu.SemaphoreType.DMA(()),
        ],
        compiler_params=pltpu.CompilerParams(vmem_limit_bytes=4 * MIB),
        name="pick",
    )(in_hbm(lists), in_hbm(tiled))


def local_part(columns, tiled, space_tiles, tree, plan):
    own, nodes, species = tiled.shape
    stored = columns.shape[0]
    slots = plan.slots
    blocks = own // LOCAL_BLOCK
    block = LOCAL_BLOCK * nodes

    def kernel(columns_hbm, x_ref, a_hbm, tree_hbm, product_hbm, p_ref, v_ref, quad_ref, meta_ref, *scratch):
        columns_ref, a_ref, tree_ref, xs_ref, c_sem, a_sem, t_sem, p_sem = scratch
        device = lax.axis_index("space")

        def load(hbm, ref, sems, b):
            at = pl.ds(b * LOCAL_BLOCK, LOCAL_BLOCK)
            return pltpu.make_async_copy(hbm.at[at], ref.at[at], sems.at[b])

        def store(b):
            return load(p_ref, product_hbm, p_sem, b)

        load_columns = pltpu.make_async_copy(columns_hbm, columns_ref, c_sem)
        load_tree = pltpu.make_async_copy(tree_hbm, tree_ref, t_sem)
        load_columns.start()
        load_tree.start()
        for b in range(blocks):
            load(a_hbm, a_ref, a_sem, b).start()

        def clear(i, _):
            v_ref[i] = jnp.zeros((nodes, species), jnp.float32)
            return 0

        lax.fori_loop(0, slots + 1, clear, 0)
        xs_ref[own] = jnp.zeros((nodes, 2 * species), jnp.bfloat16)

        def prepare(b, _):
            at = pl.ds(b * LOCAL_BLOCK, LOCAL_BLOCK)
            xs_ref[at] = side_by_side(x_ref[at].reshape(block, species)).reshape(LOCAL_BLOCK, nodes, 2 * species)
            return 0

        lax.fori_loop(0, blocks, prepare, 0)
        load_columns.wait()
        load_tree.wait()
        forward = tree_forward(tree_ref[...])

        def rows(b, carry):
            remote, quad = carry
            load(a_hbm, a_ref, a_sem, b).wait()
            parts = []
            for u in range(LOCAL_BLOCK):
                t = b * LOCAL_BLOCK + u
                tiles, last = [], jnp.int32(0)
                for k in range(stored):
                    column = columns_ref[k, t]
                    last = jnp.maximum(last, column)
                    tiles.append(xs_ref[jnp.minimum(column, own)])
                meta_ref[0, remote] = t
                remote = remote + (last >= own).astype(jnp.int32)
                parts.append(quarters(dot(stacked(a_ref[t]), jnp.concatenate(tiles, axis=0), ((1,), (0,)))))
            product = halves(dot(side_by_side(jnp.concatenate(parts, axis=0)), forward, ((1,), (1,))))
            at = pl.ds(b * LOCAL_BLOCK, LOCAL_BLOCK)
            p_ref[at] = product.reshape(LOCAL_BLOCK, nodes, species)
            store(b).start()
            x = x_ref[at].reshape(block, species)
            return remote, quad + (x * product).reshape(-1, 8, species).sum(axis=0)

        remote, quad = lax.fori_loop(0, blocks, rows, (jnp.int32(0), jnp.zeros((8, species), jnp.float32)))
        quad_ref[...] = quad
        last_row = meta_ref[0, jnp.maximum(remote - 1, 0)]
        for u in range(BLOCK):
            meta_ref[0, remote + u] = last_row
        meta_ref[1 + stored, 0] = remote
        backward = tree_backward(tree_ref[...])

        def remote_rows(b, _):
            rows = [meta_ref[0, b * BLOCK + u] for u in range(BLOCK)]
            x = jnp.concatenate([xs_ref[t] for t in rows], axis=0)
            z = side_by_side(halves(dot(x, backward, ((1,), (0,)))))
            for u, t in enumerate(rows):
                i = b * BLOCK + u
                mine = z[u * nodes : (u + 1) * nodes]
                w = halves(dot(stacked(a_ref[t]), jnp.concatenate([mine, mine], axis=0), ((0,), (0,))))
                for k in range(stored):
                    slot = plan.slot(columns_ref[k, t], own, device)
                    slot = jnp.where(i < remote, slot, slots)
                    meta_ref[1 + k, i] = slot
                    v_ref[slot] += w[k * nodes : (k + 1) * nodes]
            return 0

        lax.fori_loop(0, (remote + BLOCK - 1) // BLOCK, remote_rows, 0)
        for b in range(blocks):
            store(b).wait()

    return pl.pallas_call(
        kernel,
        out_shape=[
            pltpu.HBM(tiled.shape, jnp.float32),
            pltpu.VMEM(tiled.shape, jnp.float32),
            pltpu.VMEM((slots + 1, nodes, species), jnp.float32),
            pltpu.VMEM((8, species), jnp.float32),
            pltpu.SMEM((stored + 2, own + BLOCK), jnp.int32),
        ],
        in_specs=[HBM, VMEM, HBM, HBM],
        out_specs=[HBM, VMEM, VMEM, VMEM, SMEM],
        scratch_shapes=[
            pltpu.SMEM(columns.shape, jnp.int32),
            pltpu.VMEM(space_tiles.shape, jnp.float32),
            pltpu.VMEM(tree.shape, jnp.float32),
            pltpu.VMEM((own + 1, nodes, 2 * species), jnp.bfloat16),
            pltpu.SemaphoreType.DMA(()),
            pltpu.SemaphoreType.DMA((blocks,)),
            pltpu.SemaphoreType.DMA(()),
            pltpu.SemaphoreType.DMA((blocks,)),
        ],
        compiler_params=pltpu.CompilerParams(vmem_limit_bytes=16 * MIB),
        name="local_part",
    )(in_hbm(columns), tiled, in_hbm(space_tiles), in_hbm(tree))


def remote_quad(v, quad, received, count):
    species = v.shape[2]
    cap = received[0].shape[0]

    def kernel(v_ref, quad_ref, *rest):
        parts, out_ref = rest[:-1], rest[-1]
        total = quad_ref[...]
        for i, part in enumerate(parts):
            for j in range(cap):
                total = total + (v_ref[i * cap + j] * part[j]).reshape(-1, 8, species).sum(axis=0)
        total = total.sum(axis=0, keepdims=True)
        for i in range(count):
            out_ref[i] = total

    return pl.pallas_call(
        kernel,
        out_shape=pltpu.VMEM((count, 1, species), jnp.float32),
        in_specs=[VMEM] * (2 + len(received)),
        out_specs=VMEM,
        compiler_params=pltpu.CompilerParams(vmem_limit_bytes=8 * MIB),
        name="remote_quad",
    )(v, quad, *received)


def remote_part(meta, space_tiles, tree, local, product, received):
    own, nodes, species = product.shape
    stored = meta.shape[0] - 2
    legs, cap = len(received), received[0].shape[0]
    slots = legs * cap

    def kernel(meta_ref, tree_hbm, a_hbm, p_ref, *rest):
        parts = rest[:legs]
        _, out_hbm, tree_ref, a_ref, xs_ref, o_ref, t_sem, a_sem, sem = rest[legs:]
        remote = meta_ref[1 + stored, 0]
        padded = (remote + BLOCK - 1) // BLOCK * BLOCK

        def load(i):
            return pltpu.make_async_copy(a_hbm.at[meta_ref[0, i]], a_ref.at[i], a_sem.at[i])

        def begin(i, _):
            load(i).start()
            return 0

        load_tree = pltpu.make_async_copy(tree_hbm, tree_ref, t_sem)
        load_tree.start()
        lax.fori_loop(0, padded, begin, 0)
        xs_ref[slots] = jnp.zeros((nodes, 2 * species), jnp.bfloat16)
        for i in range(legs):
            x = parts[i][...].reshape(cap * nodes, species)
            xs_ref[i * cap : (i + 1) * cap] = side_by_side(x).reshape(cap, nodes, 2 * species)
        load_tree.wait()
        forward = tree_forward(tree_ref[...])

        def store(i):
            return pltpu.make_async_copy(o_ref.at[i], out_hbm.at[meta_ref[0, i]], sem.at[i])

        def work(b, _):
            sums = []
            for u in range(BLOCK):
                i = b * BLOCK + u
                tiles = [xs_ref[meta_ref[1 + k, i]] for k in range(stored)]
                load(i).wait()
                a = stacked(a_ref[i])
                sums.append(quarters(dot(a, jnp.concatenate(tiles, axis=0), ((1,), (0,)))))
            added = halves(dot(side_by_side(jnp.concatenate(sums, axis=0)), forward, ((1,), (1,))))
            for u in range(BLOCK):
                i = b * BLOCK + u
                o_ref[i] = p_ref[meta_ref[0, i]] + added[u * nodes : (u + 1) * nodes]

                @pl.when(i < remote)
                def _():
                    store(i).start()

            return 0

        lax.fori_loop(0, padded // BLOCK, work, 0)

        def finish(i, _):
            store(i).wait()
            return 0

        lax.fori_loop(0, remote, finish, 0)

    return pl.pallas_call(
        kernel,
        out_shape=pltpu.HBM(product.shape, jnp.float32),
        in_specs=[SMEM, HBM, HBM] + [VMEM] * (1 + legs) + [HBM],
        out_specs=HBM,
        scratch_shapes=[
            pltpu.VMEM(tree.shape, jnp.float32),
            pltpu.VMEM((own + BLOCK,) + space_tiles.shape[1:], jnp.float32),
            pltpu.VMEM((slots + 1, nodes, 2 * species), jnp.bfloat16),
            pltpu.VMEM((own + BLOCK, nodes, species), jnp.float32),
            pltpu.SemaphoreType.DMA(()),
            pltpu.SemaphoreType.DMA((own + BLOCK,)),
            pltpu.SemaphoreType.DMA((own,)),
        ],
        input_output_aliases={4 + legs: 0},
        compiler_params=pltpu.CompilerParams(vmem_limit_bytes=16 * MIB),
        name="remote_part",
    )(meta, in_hbm(tree), in_hbm(space_tiles), local, *received, in_hbm(product))


def on_device(signal, space_tiles, tree_precision, send_tiles, column_tiles):
    count = lax.axis_size("space")
    tile_rows, tile_nodes = space_tiles.shape[:2]
    species = signal.shape[1]
    plan = Exchange(count, send_tiles.shape[2])
    tiled = signal.reshape(tile_rows, tile_nodes, species)
    *outgoing, tiled = pick(send_tiles, tiled, plan)
    received = [lax.ppermute(o, "space", plan.route(leg)) for o, leg in zip(outgoing, plan.legs)]
    product, local, v, quad, meta = local_part(column_tiles.T, tiled, space_tiles, tree_precision, plan)
    shares = remote_quad(v, quad, received, count)
    sums = lax.all_to_all(shares, "space", 0, 0)
    product = remote_part(meta, space_tiles, tree_precision, local, product, received)
    scale = 1.0 / math.sqrt(count * tile_rows * tile_nodes * species)
    return product.reshape(signal.shape), (jnp.sum(sums) * scale).reshape(1)


def solution(mesh):
    placed = (
        P(("groups", "space"), None),
        P("space", None, None),
        P("groups", None),
        P("space", None, None),
        P("space", None),
    )
    return jax.shard_map(
        on_device,
        mesh=mesh,
        in_specs=placed,
        out_specs=(P(("groups", "space"), None), P("groups")),
        check_vma=False,
    )
```

```python
import math

import jax
import jax.numpy as jnp
from jax import lax
from jax.experimental import pallas as pl
from jax.experimental.pallas import tpu as pltpu
from jax.sharding import PartitionSpec as P

ROWS = 8
LOCAL_BLOCK = 8
BLOCK = 4
HBM = pl.BlockSpec(memory_space=pltpu.HBM)
SMEM = pl.BlockSpec(memory_space=pltpu.SMEM)
VMEM = pl.BlockSpec(memory_space=pltpu.VMEM)
MIB = 1024 * 1024


def in_hbm(x):
    return pltpu.with_memory_space_constraint(x, pltpu.HBM)


def split(x):
    high = x.astype(jnp.bfloat16)
    return high, (x - high.astype(jnp.float32)).astype(jnp.bfloat16)


def stacked(x):
    return jnp.concatenate(split(x), axis=0)


def side_by_side(x):
    return jnp.concatenate(split(x), axis=1)


def dot(a, b, dims):
    return lax.dot_general(a, b, (dims, ((), ())), preferred_element_type=jnp.float32)


def quarters(s):
    rows, lanes = s.shape[0] // 2, s.shape[1] // 2
    return (s[rows:, lanes:] + s[rows:, :lanes]) + s[:rows, lanes:] + s[:rows, :lanes]


def halves(s):
    lanes = s.shape[1] // 2
    return s[:, lanes:] + s[:, :lanes]


def tree_forward(tree):
    rows = stacked(tree)
    return jnp.concatenate([rows, rows], axis=1)


def tree_backward(tree):
    lanes = side_by_side(tree)
    return jnp.concatenate([lanes, lanes], axis=0)


class Exchange:
    def __init__(self, count, cap):
        self.count, self.cap = count, cap
        self.wide = count // ROWS
        self.legs = [(self.wide, 0, 2, 3)]
        if ROWS > 2:
            self.legs.append((self.wide, 1, 2, 3))
        if self.wide > 1:
            self.legs.append((1, 0, 0, 1))
        if self.wide > 2:
            self.legs.append((1, 1, 0, 1))
        self.slots = len(self.legs) * cap

    def place(self, device, step):
        return device // self.wide if step == self.wide else device % self.wide

    def extent(self, step):
        return ROWS if step == self.wide else self.wide

    def route(self, leg):
        step, odd = leg[:2]
        pairs = []
        for i in range(self.count):
            at = self.place(i, step)
            if at % 2 == odd and at + 1 < self.extent(step):
                pairs += [(i, i + step), (i + step, i)]
        return pairs

    def sends(self, leg, device):
        step, odd, up, down = leg
        return jnp.where(self.place(device, step) % 2 == odd, up, down)

    def slot(self, column, own, device):
        entry = column - own
        direction = entry // self.cap
        base = jnp.int32(0)
        for i, leg in enumerate(self.legs):
            base = jnp.where(direction == leg[2] + leg[3] - self.sends(leg, device), i * self.cap, base)
        return jnp.where(entry < 0, self.slots, base + entry % self.cap)


def pick(lists, tiled, plan):
    cap, legs = plan.cap, plan.legs
    chunks = 4
    chunk = tiled.shape[0] // chunks
    shape = pltpu.VMEM((cap,) + tiled.shape[1:], tiled.dtype)

    def kernel(lists_hbm, tiled_hbm, *rest):
        outs, tiled_ref = rest[: len(legs)], rest[len(legs)]
        lists_ref, sems, sem = rest[len(legs) + 1 :]
        loads = [pltpu.make_async_copy(lists_hbm, lists_ref, sem)]
        for i in range(chunks):
            at = pl.ds(i * chunk, chunk)
            loads.append(pltpu.make_async_copy(tiled_hbm.at[at], tiled_ref.at[at], sems.at[i]))
        for load in loads:
            load.start()
        device = lax.axis_index("space")
        directions = [plan.sends(leg, device) for leg in legs]
        for load in loads:
            load.wait()
        for i, direction in enumerate(directions):
            for j in range(cap):
                outs[i][j] = tiled_ref[lists_ref[0, direction, j]]

    return pl.pallas_call(
        kernel,
        out_shape=[shape] * len(legs) + [pltpu.VMEM(tiled.shape, tiled.dtype)],
        in_specs=[HBM, HBM],
        out_specs=[VMEM] * (len(legs) + 1),
        scratch_shapes=[
            pltpu.SMEM(lists.shape, jnp.int32),
            pltpu.SemaphoreType.DMA((chunks,)),
            pltpu.SemaphoreType.DMA(()),
        ],
        compiler_params=pltpu.CompilerParams(vmem_limit_bytes=4 * MIB),
        name="pick",
    )(in_hbm(lists), in_hbm(tiled))


def local_part(columns, tiled, space_tiles, tree, plan):
    own, nodes, species = tiled.shape
    stored = columns.shape[0]
    slots = plan.slots
    blocks = own // LOCAL_BLOCK
    block = LOCAL_BLOCK * nodes

    def kernel(columns_hbm, x_ref, a_hbm, tree_hbm, product_hbm, *rest):
        p_ref, v_ref, quad_ref, meta_ref, forward_ref, a_ref = rest[:6]
        columns_ref, tree_ref, xs_ref, c_sem, a_sem, t_sem, p_sem = rest[6:]
        device = lax.axis_index("space")

        def load(hbm, ref, sems, b):
            at = pl.ds(b * LOCAL_BLOCK, LOCAL_BLOCK)
            return pltpu.make_async_copy(hbm.at[at], ref.at[at], sems.at[b])

        def store(b):
            return load(p_ref, product_hbm, p_sem, b)

        load_columns = pltpu.make_async_copy(columns_hbm, columns_ref, c_sem)
        load_tree = pltpu.make_async_copy(tree_hbm, tree_ref, t_sem)
        load_columns.start()
        load_tree.start()
        for b in range(blocks):
            load(a_hbm, a_ref, a_sem, b).start()

        def clear(i, _):
            v_ref[i] = jnp.zeros((nodes, species), jnp.float32)
            return 0

        lax.fori_loop(0, slots + 1, clear, 0)
        xs_ref[own] = jnp.zeros((nodes, 2 * species), jnp.bfloat16)

        def prepare(b, _):
            at = pl.ds(b * LOCAL_BLOCK, LOCAL_BLOCK)
            xs_ref[at] = side_by_side(x_ref[at].reshape(block, species)).reshape(LOCAL_BLOCK, nodes, 2 * species)
            return 0

        lax.fori_loop(0, blocks, prepare, 0)
        load_columns.wait()
        load_tree.wait()
        forward = tree_forward(tree_ref[...])
        forward_ref[...] = forward

        def rows(b, carry):
            remote, quad = carry
            load(a_hbm, a_ref, a_sem, b).wait()
            parts = []
            for u in range(LOCAL_BLOCK):
                t = b * LOCAL_BLOCK + u
                tiles, last = [], jnp.int32(0)
                for k in range(stored):
                    column = columns_ref[k, t]
                    last = jnp.maximum(last, column)
                    tiles.append(xs_ref[jnp.minimum(column, own)])
                meta_ref[0, remote] = t
                remote = remote + (last >= own).astype(jnp.int32)
                parts.append(quarters(dot(stacked(a_ref[t]), jnp.concatenate(tiles, axis=0), ((1,), (0,)))))
            product = halves(dot(side_by_side(jnp.concatenate(parts, axis=0)), forward, ((1,), (1,))))
            at = pl.ds(b * LOCAL_BLOCK, LOCAL_BLOCK)
            p_ref[at] = product.reshape(LOCAL_BLOCK, nodes, species)
            store(b).start()
            x = x_ref[at].reshape(block, species)
            return remote, quad + (x * product).reshape(-1, 8, species).sum(axis=0)

        remote, quad = lax.fori_loop(0, blocks, rows, (jnp.int32(0), jnp.zeros((8, species), jnp.float32)))
        quad_ref[...] = quad
        last_row = meta_ref[0, jnp.maximum(remote - 1, 0)]
        for u in range(BLOCK):
            meta_ref[0, remote + u] = last_row
        meta_ref[1 + stored, 0] = remote
        backward = tree_backward(tree_ref[...])

        def remote_rows(b, _):
            rows = [meta_ref[0, b * BLOCK + u] for u in range(BLOCK)]
            x = jnp.concatenate([xs_ref[t] for t in rows], axis=0)
            z = side_by_side(halves(dot(x, backward, ((1,), (0,)))))
            for u, t in enumerate(rows):
                i = b * BLOCK + u
                mine = z[u * nodes : (u + 1) * nodes]
                w = halves(dot(stacked(a_ref[t]), jnp.concatenate([mine, mine], axis=0), ((0,), (0,))))
                for k in range(stored):
                    slot = plan.slot(columns_ref[k, t], own, device)
                    slot = jnp.where(i < remote, slot, slots)
                    meta_ref[1 + k, i] = slot
                    v_ref[slot] += w[k * nodes : (k + 1) * nodes]
            return 0

        lax.fori_loop(0, (remote + BLOCK - 1) // BLOCK, remote_rows, 0)
        for b in range(blocks):
            store(b).wait()

    return pl.pallas_call(
        kernel,
        out_shape=[
            pltpu.HBM(tiled.shape, jnp.float32),
            pltpu.VMEM(tiled.shape, jnp.float32),
            pltpu.VMEM((slots + 1, nodes, species), jnp.float32),
            pltpu.VMEM((8, species), jnp.float32),
            pltpu.SMEM((stored + 2, own + BLOCK), jnp.int32),
            pltpu.VMEM((2 * species, 2 * species), jnp.bfloat16),
            pltpu.VMEM(space_tiles.shape, jnp.float32),
        ],
        in_specs=[HBM, VMEM, HBM, HBM],
        out_specs=[HBM, VMEM, VMEM, VMEM, SMEM, VMEM, VMEM],
        scratch_shapes=[
            pltpu.SMEM(columns.shape, jnp.int32),
            pltpu.VMEM(tree.shape, jnp.float32),
            pltpu.VMEM((own + 1, nodes, 2 * species), jnp.bfloat16),
            pltpu.SemaphoreType.DMA(()),
            pltpu.SemaphoreType.DMA((blocks,)),
            pltpu.SemaphoreType.DMA(()),
            pltpu.SemaphoreType.DMA((blocks,)),
        ],
        compiler_params=pltpu.CompilerParams(vmem_limit_bytes=16 * MIB),
        name="local_part",
    )(in_hbm(columns), tiled, in_hbm(space_tiles), in_hbm(tree))


def remote_quad(v, quad, received):
    species = v.shape[2]
    cap = received[0].shape[0]

    def kernel(v_ref, quad_ref, *rest):
        parts, out_ref = rest[:-1], rest[-1]
        total = quad_ref[...]
        for i, part in enumerate(parts):
            for j in range(cap):
                total = total + (v_ref[i * cap + j] * part[j]).reshape(-1, 8, species).sum(axis=0)
        out_ref[...] = total.sum(axis=0, keepdims=True)

    return pl.pallas_call(
        kernel,
        out_shape=pltpu.VMEM((1, species), jnp.float32),
        in_specs=[VMEM] * (2 + len(received)),
        out_specs=VMEM,
        compiler_params=pltpu.CompilerParams(vmem_limit_bytes=8 * MIB),
        name="remote_quad",
    )(v, quad, *received)


def swap_rounds(count):
    masks = [1 << bit for bit in range(count.bit_length() - 1)]
    if 1 << len(masks) != count or len(masks) < 4:
        return []
    return [masks[-1:], [1, 2, 3]] + [[mask] for mask in masks[-2:1:-1]]


def swap_sum(x, count, beside):
    rounds = swap_rounds(count)
    if not rounds:
        return lax.psum(x, "space"), jnp.zeros_like(x), beside
    for i, masks in enumerate(rounds):
        others = [lax.ppermute(x, "space", [(j, j ^ mask) for j in range(count)]) for mask in masks]
        if i == len(rounds) - 1:
            return x, others[0], beside
        x = x + others[0]
        if len(others) == 3:
            x = x + (others[1] + others[2])
        if i == 0:
            x, beside = lax.optimization_barrier((x, beside))


def remote_part(meta, space_tiles, forward, local, received):
    own, nodes, species = local.shape
    stored = meta.shape[0] - 2
    legs, cap = len(received), received[0].shape[0]
    slots = legs * cap

    def kernel(meta_ref, forward_ref, a_ref, p_ref, *rest):
        parts, (o_ref, xs_ref) = rest[:legs], rest[legs:]
        xs_ref[slots] = jnp.zeros((nodes, 2 * species), jnp.bfloat16)
        for i in range(legs):
            x = parts[i][...].reshape(cap * nodes, species)
            xs_ref[i * cap : (i + 1) * cap] = side_by_side(x).reshape(cap, nodes, 2 * species)
        forward = forward_ref[...]

        def work(b, _):
            rows = [meta_ref[0, b * BLOCK + u] for u in range(BLOCK)]
            sums = []
            for u, t in enumerate(rows):
                tiles = [xs_ref[meta_ref[1 + k, b * BLOCK + u]] for k in range(stored)]
                sums.append(quarters(dot(stacked(a_ref[t]), jnp.concatenate(tiles, axis=0), ((1,), (0,)))))
            added = halves(dot(side_by_side(jnp.concatenate(sums, axis=0)), forward, ((1,), (1,))))
            for u, t in enumerate(rows):
                o_ref[b * BLOCK + u] = p_ref[t] + added[u * nodes : (u + 1) * nodes]
            return 0

        lax.fori_loop(0, (meta_ref[1 + stored, 0] + BLOCK - 1) // BLOCK, work, 0)

    return pl.pallas_call(
        kernel,
        out_shape=pltpu.VMEM((own + BLOCK, nodes, species), jnp.float32),
        in_specs=[SMEM] + [VMEM] * (3 + legs),
        out_specs=VMEM,
        scratch_shapes=[pltpu.VMEM((slots + 1, nodes, 2 * species), jnp.bfloat16)],
        compiler_params=pltpu.CompilerParams(vmem_limit_bytes=16 * MIB),
        name="remote_part",
    )(meta, forward, space_tiles, local, *received)


def store(meta, changed, product):
    own = product.shape[0]
    stored = meta.shape[0] - 2

    def kernel(meta_ref, changed_ref, _, product_hbm, sems):
        remote = meta_ref[1 + stored, 0]

        def copy(i):
            return pltpu.make_async_copy(changed_ref.at[i], product_hbm.at[meta_ref[0, i]], sems.at[i])

        def begin(i, _):
            copy(i).start()
            return 0

        def end(i, _):
            copy(i).wait()
            return 0

        lax.fori_loop(0, remote, begin, 0)
        lax.fori_loop(0, remote, end, 0)

    return pl.pallas_call(
        kernel,
        out_shape=pltpu.HBM(product.shape, jnp.float32),
        in_specs=[SMEM, VMEM, HBM],
        out_specs=HBM,
        scratch_shapes=[pltpu.SemaphoreType.DMA((own,))],
        input_output_aliases={2: 0},
        compiler_params=pltpu.CompilerParams(vmem_limit_bytes=8 * MIB),
        name="store",
    )(meta, changed, in_hbm(product))


def finish(x, y, scale):
    def kernel(x_ref, y_ref, quad_ref):
        quad_ref[0] = jnp.sum(x_ref[...] + y_ref[...]) * scale

    return pl.pallas_call(
        kernel,
        out_shape=jax.ShapeDtypeStruct((1,), jnp.float32),
        in_specs=[VMEM, VMEM],
        out_specs=SMEM,
        compiler_params=pltpu.CompilerParams(vmem_limit_bytes=MIB),
        name="finish",
    )(x, y)


def on_device(signal, space_tiles, tree_precision, send_tiles, column_tiles):
    count = lax.axis_size("space")
    tile_rows, tile_nodes = space_tiles.shape[:2]
    species = signal.shape[1]
    plan = Exchange(count, send_tiles.shape[2])
    tiled = signal.reshape(tile_rows, tile_nodes, species)
    *outgoing, tiled = pick(send_tiles, tiled, plan)
    received = [lax.ppermute(o, "space", plan.route(leg)) for o, leg in zip(outgoing, plan.legs)]
    product, local, v, quad, meta, forward, space_tiles = local_part(
        column_tiles.T, tiled, space_tiles, tree_precision, plan
    )
    share = remote_quad(v, quad, received)
    changed = remote_part(meta, space_tiles, forward, local, received)
    x, y, changed = swap_sum(share, count, changed)
    product = store(meta, changed, product)
    scale = 1.0 / math.sqrt(count * tile_rows * tile_nodes * species)
    return product.reshape(signal.shape), finish(x, y, scale)


def solution(mesh):
    placed = (
        P(("groups", "space"), None),
        P("space", None, None),
        P("groups", None),
        P("space", None, None),
        P("space", None),
    )
    return jax.shard_map(
        on_device,
        mesh=mesh,
        in_specs=placed,
        out_specs=(P(("groups", "space"), None), P("groups")),
        check_vma=False,
    )
```

```python
import math

import jax
import jax.numpy as jnp
from jax import lax
from jax.experimental import pallas as pl
from jax.experimental.pallas import tpu as pltpu
from jax.sharding import PartitionSpec as P

ROWS = 8
LOCAL_BLOCK = 8
BLOCK = 4
HBM = pl.BlockSpec(memory_space=pltpu.HBM)
SMEM = pl.BlockSpec(memory_space=pltpu.SMEM)
VMEM = pl.BlockSpec(memory_space=pltpu.VMEM)
MIB = 1024 * 1024


def in_hbm(x):
    return pltpu.with_memory_space_constraint(x, pltpu.HBM)


def split(x):
    high = x.astype(jnp.bfloat16)
    return high, (x - high.astype(jnp.float32)).astype(jnp.bfloat16)


def stacked(x):
    return jnp.concatenate(split(x), axis=0)


def side_by_side(x):
    return jnp.concatenate(split(x), axis=1)


def dot(a, b, dims):
    return lax.dot_general(a, b, (dims, ((), ())), preferred_element_type=jnp.float32)


def quarters(s):
    rows, lanes = s.shape[0] // 2, s.shape[1] // 2
    return (s[rows:, lanes:] + s[rows:, :lanes]) + s[:rows, lanes:] + s[:rows, :lanes]


def halves(s):
    lanes = s.shape[1] // 2
    return s[:, lanes:] + s[:, :lanes]


def tree_forward(tree):
    rows = stacked(tree)
    return jnp.concatenate([rows, rows], axis=1)


def tree_backward(tree):
    lanes = side_by_side(tree)
    return jnp.concatenate([lanes, lanes], axis=0)


class Exchange:
    def __init__(self, count, cap):
        self.count, self.cap = count, cap
        self.wide = count // ROWS
        self.legs = [(self.wide, 0, 2, 3)]
        if ROWS > 2:
            self.legs.append((self.wide, 1, 2, 3))
        if self.wide > 1:
            self.legs.append((1, 0, 0, 1))
        if self.wide > 2:
            self.legs.append((1, 1, 0, 1))
        self.slots = len(self.legs) * cap

    def place(self, device, step):
        return device // self.wide if step == self.wide else device % self.wide

    def extent(self, step):
        return ROWS if step == self.wide else self.wide

    def route(self, leg):
        step, odd = leg[:2]
        pairs = []
        for i in range(self.count):
            at = self.place(i, step)
            if at % 2 == odd and at + 1 < self.extent(step):
                pairs += [(i, i + step), (i + step, i)]
        return pairs

    def sends(self, leg, device):
        step, odd, up, down = leg
        return jnp.where(self.place(device, step) % 2 == odd, up, down)

    def slot(self, column, own, device):
        entry = column - own
        direction = entry // self.cap
        base = jnp.int32(0)
        for i, leg in enumerate(self.legs):
            base = jnp.where(direction == leg[2] + leg[3] - self.sends(leg, device), i * self.cap, base)
        return jnp.where(entry < 0, self.slots, base + entry % self.cap)


def pick(lists, tiled, plan):
    cap, legs = plan.cap, plan.legs
    chunks = 4
    chunk = tiled.shape[0] // chunks
    shape = pltpu.VMEM((cap,) + tiled.shape[1:], tiled.dtype)

    def kernel(lists_hbm, tiled_hbm, *rest):
        outs, tiled_ref = rest[: len(legs)], rest[len(legs)]
        lists_ref, sems, sem = rest[len(legs) + 1 :]
        loads = [pltpu.make_async_copy(lists_hbm, lists_ref, sem)]
        for i in range(chunks):
            at = pl.ds(i * chunk, chunk)
            loads.append(pltpu.make_async_copy(tiled_hbm.at[at], tiled_ref.at[at], sems.at[i]))
        for load in loads:
            load.start()
        device = lax.axis_index("space")
        directions = [plan.sends(leg, device) for leg in legs]
        for load in loads:
            load.wait()
        for i, direction in enumerate(directions):
            for j in range(cap):
                outs[i][j] = tiled_ref[lists_ref[0, direction, j]]

    return pl.pallas_call(
        kernel,
        out_shape=[shape] * len(legs) + [pltpu.VMEM(tiled.shape, tiled.dtype)],
        in_specs=[HBM, HBM],
        out_specs=[VMEM] * (len(legs) + 1),
        scratch_shapes=[
            pltpu.SMEM(lists.shape, jnp.int32),
            pltpu.SemaphoreType.DMA((chunks,)),
            pltpu.SemaphoreType.DMA(()),
        ],
        compiler_params=pltpu.CompilerParams(vmem_limit_bytes=4 * MIB),
        name="pick",
    )(in_hbm(lists), in_hbm(tiled))


def local_part(columns, tiled, space_tiles, tree, plan):
    own, nodes, species = tiled.shape
    stored = columns.shape[0]
    slots = plan.slots
    blocks = own // LOCAL_BLOCK
    block = LOCAL_BLOCK * nodes

    def kernel(columns_hbm, x_ref, a_hbm, tree_hbm, product_hbm, *rest):
        p_ref, v_ref, quad_ref, meta_ref, forward_ref, a_ref = rest[:6]
        columns_ref, tree_ref, xs_ref, c_sem, a_sem, t_sem, p_sem = rest[6:]
        device = lax.axis_index("space")

        def load(hbm, ref, sems, b):
            at = pl.ds(b * LOCAL_BLOCK, LOCAL_BLOCK)
            return pltpu.make_async_copy(hbm.at[at], ref.at[at], sems.at[b])

        def store(b):
            return load(p_ref, product_hbm, p_sem, b)

        load_columns = pltpu.make_async_copy(columns_hbm, columns_ref, c_sem)
        load_tree = pltpu.make_async_copy(tree_hbm, tree_ref, t_sem)
        load_columns.start()
        load_tree.start()
        for b in range(blocks):
            load(a_hbm, a_ref, a_sem, b).start()

        def clear(i, _):
            v_ref[i] = jnp.zeros((nodes, species), jnp.float32)
            return 0

        lax.fori_loop(0, slots + 1, clear, 0)
        xs_ref[own] = jnp.zeros((nodes, 2 * species), jnp.bfloat16)

        def prepare(b, _):
            at = pl.ds(b * LOCAL_BLOCK, LOCAL_BLOCK)
            xs_ref[at] = side_by_side(x_ref[at].reshape(block, species)).reshape(LOCAL_BLOCK, nodes, 2 * species)
            return 0

        lax.fori_loop(0, blocks, prepare, 0)
        load_columns.wait()
        load_tree.wait()
        forward = tree_forward(tree_ref[...])
        forward_ref[...] = forward

        def rows(b, carry):
            remote, quad = carry
            load(a_hbm, a_ref, a_sem, b).wait()
            parts = []
            for u in range(LOCAL_BLOCK):
                t = b * LOCAL_BLOCK + u
                tiles, last = [], jnp.int32(0)
                for k in range(stored):
                    column = columns_ref[k, t]
                    last = jnp.maximum(last, column)
                    tiles.append(xs_ref[jnp.minimum(column, own)])
                meta_ref[0, remote] = t
                remote = remote + (last >= own).astype(jnp.int32)
                parts.append(quarters(dot(stacked(a_ref[t]), jnp.concatenate(tiles, axis=0), ((1,), (0,)))))
            product = halves(dot(side_by_side(jnp.concatenate(parts, axis=0)), forward, ((1,), (1,))))
            at = pl.ds(b * LOCAL_BLOCK, LOCAL_BLOCK)
            p_ref[at] = product.reshape(LOCAL_BLOCK, nodes, species)
            store(b).start()
            x = x_ref[at].reshape(block, species)
            return remote, quad + (x * product).reshape(-1, 8, species).sum(axis=0)

        remote, quad = lax.fori_loop(0, blocks, rows, (jnp.int32(0), jnp.zeros((8, species), jnp.float32)))
        quad_ref[...] = quad
        last_row = meta_ref[0, jnp.maximum(remote - 1, 0)]
        for u in range(BLOCK):
            meta_ref[0, remote + u] = last_row
        meta_ref[1 + stored, 0] = remote
        backward = tree_backward(tree_ref[...])

        def remote_rows(b, _):
            rows = [meta_ref[0, b * BLOCK + u] for u in range(BLOCK)]
            x = jnp.concatenate([xs_ref[t] for t in rows], axis=0)
            z = side_by_side(halves(dot(x, backward, ((1,), (0,)))))
            for u, t in enumerate(rows):
                i = b * BLOCK + u
                mine = z[u * nodes : (u + 1) * nodes]
                w = halves(dot(stacked(a_ref[t]), jnp.concatenate([mine, mine], axis=0), ((0,), (0,))))
                for k in range(stored):
                    slot = plan.slot(columns_ref[k, t], own, device)
                    slot = jnp.where(i < remote, slot, slots)
                    meta_ref[1 + k, i] = slot
                    v_ref[slot] += w[k * nodes : (k + 1) * nodes]
            return 0

        lax.fori_loop(0, (remote + BLOCK - 1) // BLOCK, remote_rows, 0)
        for b in range(blocks):
            store(b).wait()

    return pl.pallas_call(
        kernel,
        out_shape=[
            pltpu.HBM(tiled.shape, jnp.float32),
            pltpu.VMEM(tiled.shape, jnp.float32),
            pltpu.VMEM((slots + 1, nodes, species), jnp.float32),
            pltpu.VMEM((8, species), jnp.float32),
            pltpu.SMEM((stored + 2, own + BLOCK), jnp.int32),
            pltpu.VMEM((2 * species, 2 * species), jnp.bfloat16),
            pltpu.VMEM(space_tiles.shape, jnp.float32),
        ],
        in_specs=[HBM, VMEM, HBM, HBM],
        out_specs=[HBM, VMEM, VMEM, VMEM, SMEM, VMEM, VMEM],
        scratch_shapes=[
            pltpu.SMEM(columns.shape, jnp.int32),
            pltpu.VMEM(tree.shape, jnp.float32),
            pltpu.VMEM((own + 1, nodes, 2 * species), jnp.bfloat16),
            pltpu.SemaphoreType.DMA(()),
            pltpu.SemaphoreType.DMA((blocks,)),
            pltpu.SemaphoreType.DMA(()),
            pltpu.SemaphoreType.DMA((blocks,)),
        ],
        compiler_params=pltpu.CompilerParams(vmem_limit_bytes=16 * MIB),
        name="local_part",
    )(in_hbm(columns), tiled, in_hbm(space_tiles), in_hbm(tree))


def remote_quad(v, quad, received):
    species = v.shape[2]
    cap = received[0].shape[0]

    def kernel(v_ref, quad_ref, *rest):
        parts, out_ref = rest[:-1], rest[-1]
        total = quad_ref[...]
        for i, part in enumerate(parts):
            for j in range(cap):
                total = total + (v_ref[i * cap + j] * part[j]).reshape(-1, 8, species).sum(axis=0)
        out_ref[...] = total.sum(axis=0, keepdims=True)

    return pl.pallas_call(
        kernel,
        out_shape=pltpu.VMEM((1, species), jnp.float32),
        in_specs=[VMEM] * (2 + len(received)),
        out_specs=VMEM,
        compiler_params=pltpu.CompilerParams(vmem_limit_bytes=8 * MIB),
        name="remote_quad",
    )(v, quad, *received)


def swap_masks(count):
    masks = [1 << bit for bit in range(count.bit_length() - 1)]
    if 1 << len(masks) != count or len(masks) < 3:
        return []
    return [mask | 1 for mask in [masks[-1], masks[1]] + masks[-2:1:-1]] + [1]


def swap_sum(x, count, changed, put):
    masks = swap_masks(count)
    if not masks:
        return lax.psum(x, "space"), jnp.zeros_like(x), put(changed)
    for i, mask in enumerate(masks[:-1]):
        x = x + lax.ppermute(x, "space", [(j, j ^ mask) for j in range(count)])
        if i == 0:
            x, changed = lax.optimization_barrier((x, changed))
        if i == len(masks) - 2:
            x, product = lax.optimization_barrier((x, put(changed)))
    return x, lax.ppermute(x, "space", [(j, j ^ masks[-1]) for j in range(count)]), product


def remote_part(meta, space_tiles, forward, local, received):
    own, nodes, species = local.shape
    stored = meta.shape[0] - 2
    legs, cap = len(received), received[0].shape[0]
    slots = legs * cap

    def kernel(meta_ref, forward_ref, a_ref, p_ref, *rest):
        parts, (o_ref, xs_ref) = rest[:legs], rest[legs:]
        xs_ref[slots] = jnp.zeros((nodes, 2 * species), jnp.bfloat16)
        for i in range(legs):
            x = parts[i][...].reshape(cap * nodes, species)
            xs_ref[i * cap : (i + 1) * cap] = side_by_side(x).reshape(cap, nodes, 2 * species)
        forward = forward_ref[...]

        def work(b, _):
            rows = [meta_ref[0, b * BLOCK + u] for u in range(BLOCK)]
            sums = []
            for u, t in enumerate(rows):
                tiles = [xs_ref[meta_ref[1 + k, b * BLOCK + u]] for k in range(stored)]
                sums.append(quarters(dot(stacked(a_ref[t]), jnp.concatenate(tiles, axis=0), ((1,), (0,)))))
            added = halves(dot(side_by_side(jnp.concatenate(sums, axis=0)), forward, ((1,), (1,))))
            for u, t in enumerate(rows):
                o_ref[b * BLOCK + u] = p_ref[t] + added[u * nodes : (u + 1) * nodes]
            return 0

        lax.fori_loop(0, (meta_ref[1 + stored, 0] + BLOCK - 1) // BLOCK, work, 0)

    return pl.pallas_call(
        kernel,
        out_shape=pltpu.VMEM((own + BLOCK, nodes, species), jnp.float32),
        in_specs=[SMEM] + [VMEM] * (3 + legs),
        out_specs=VMEM,
        scratch_shapes=[pltpu.VMEM((slots + 1, nodes, 2 * species), jnp.bfloat16)],
        compiler_params=pltpu.CompilerParams(vmem_limit_bytes=16 * MIB),
        name="remote_part",
    )(meta, forward, space_tiles, local, *received)


def store(meta, changed, product):
    own = product.shape[0]
    stored = meta.shape[0] - 2

    def kernel(meta_ref, changed_ref, _, product_hbm, sems):
        remote = meta_ref[1 + stored, 0]

        def copy(i):
            return pltpu.make_async_copy(changed_ref.at[i], product_hbm.at[meta_ref[0, i]], sems.at[i])

        def begin(i, _):
            copy(i).start()
            return 0

        def end(i, _):
            copy(i).wait()
            return 0

        lax.fori_loop(0, remote, begin, 0)
        lax.fori_loop(0, remote, end, 0)

    return pl.pallas_call(
        kernel,
        out_shape=pltpu.HBM(product.shape, jnp.float32),
        in_specs=[SMEM, VMEM, HBM],
        out_specs=HBM,
        scratch_shapes=[pltpu.SemaphoreType.DMA((own,))],
        input_output_aliases={2: 0},
        compiler_params=pltpu.CompilerParams(vmem_limit_bytes=8 * MIB),
        name="store",
    )(meta, changed, in_hbm(product))


def finish(x, y, scale):
    def kernel(x_ref, y_ref, quad_ref):
        quad_ref[0] = jnp.sum(x_ref[...] + y_ref[...]) * scale

    return pl.pallas_call(
        kernel,
        out_shape=jax.ShapeDtypeStruct((1,), jnp.float32),
        in_specs=[VMEM, VMEM],
        out_specs=SMEM,
        compiler_params=pltpu.CompilerParams(vmem_limit_bytes=MIB),
        name="finish",
    )(x, y)


def on_device(signal, space_tiles, tree_precision, send_tiles, column_tiles):
    count = lax.axis_size("space")
    tile_rows, tile_nodes = space_tiles.shape[:2]
    species = signal.shape[1]
    plan = Exchange(count, send_tiles.shape[2])
    tiled = signal.reshape(tile_rows, tile_nodes, species)
    *outgoing, tiled = pick(send_tiles, tiled, plan)
    received = [lax.ppermute(o, "space", plan.route(leg)) for o, leg in zip(outgoing, plan.legs)]
    product, local, v, quad, meta, forward, space_tiles = local_part(
        column_tiles.T, tiled, space_tiles, tree_precision, plan
    )
    share = remote_quad(v, quad, received)
    changed = remote_part(meta, space_tiles, forward, local, received)
    x, y, product = swap_sum(share, count, changed, lambda rows: store(meta, rows, product))
    scale = 1.0 / math.sqrt(count * tile_rows * tile_nodes * species)
    return product.reshape(signal.shape), finish(x, y, scale)


def solution(mesh):
    placed = (
        P(("groups", "space"), None),
        P("space", None, None),
        P("groups", None),
        P("space", None, None),
        P("space", None),
    )
    return jax.shard_map(
        on_device,
        mesh=mesh,
        in_specs=placed,
        out_specs=(P(("groups", "space"), None), P("groups")),
        check_vma=False,
    )
```

```python
import math

import jax
import jax.numpy as jnp
from jax import lax
from jax.experimental import pallas as pl
from jax.experimental.pallas import tpu as pltpu
from jax.sharding import PartitionSpec as P

ROWS = 8
LOCAL_BLOCK = 8
BLOCK = 4
HBM = pl.BlockSpec(memory_space=pltpu.HBM)
SMEM = pl.BlockSpec(memory_space=pltpu.SMEM)
VMEM = pl.BlockSpec(memory_space=pltpu.VMEM)
MIB = 1024 * 1024


def in_hbm(x):
    return pltpu.with_memory_space_constraint(x, pltpu.HBM)


def split(x):
    high = x.astype(jnp.bfloat16)
    return high, (x - high.astype(jnp.float32)).astype(jnp.bfloat16)


def stacked(x):
    return jnp.concatenate(split(x), axis=0)


def side_by_side(x):
    return jnp.concatenate(split(x), axis=1)


def dot(a, b, dims):
    return lax.dot_general(a, b, (dims, ((), ())), preferred_element_type=jnp.float32)


def quarters(s):
    rows, lanes = s.shape[0] // 2, s.shape[1] // 2
    return (s[rows:, lanes:] + s[rows:, :lanes]) + s[:rows, lanes:] + s[:rows, :lanes]


def halves(s):
    lanes = s.shape[1] // 2
    return s[:, lanes:] + s[:, :lanes]


def tree_forward(tree):
    rows = stacked(tree)
    return jnp.concatenate([rows, rows], axis=1)


def tree_backward(tree):
    lanes = side_by_side(tree)
    return jnp.concatenate([lanes, lanes], axis=0)


class Exchange:
    def __init__(self, count, cap):
        self.count, self.cap = count, cap
        self.wide = count // ROWS
        self.legs = [(self.wide, 0, 2, 3)]
        if ROWS > 2:
            self.legs.append((self.wide, 1, 2, 3))
        if self.wide > 1:
            self.legs.append((1, 0, 0, 1))
        if self.wide > 2:
            self.legs.append((1, 1, 0, 1))
        self.slots = len(self.legs) * cap

    def place(self, device, step):
        return device // self.wide if step == self.wide else device % self.wide

    def extent(self, step):
        return ROWS if step == self.wide else self.wide

    def route(self, leg):
        step, odd = leg[:2]
        pairs = []
        for i in range(self.count):
            at = self.place(i, step)
            if at % 2 == odd and at + 1 < self.extent(step):
                pairs += [(i, i + step), (i + step, i)]
        return pairs

    def sends(self, leg, device):
        step, odd, up, down = leg
        return jnp.where(self.place(device, step) % 2 == odd, up, down)

    def slot(self, column, own, device):
        entry = column - own
        direction = entry // self.cap
        base = jnp.int32(0)
        for i, leg in enumerate(self.legs):
            base = jnp.where(direction == leg[2] + leg[3] - self.sends(leg, device), i * self.cap, base)
        return jnp.where(entry < 0, self.slots, base + entry % self.cap)


def pick(lists, tiled, plan):
    cap, legs = plan.cap, plan.legs
    chunks = 4
    chunk = tiled.shape[0] // chunks
    shape = pltpu.VMEM((cap,) + tiled.shape[1:], tiled.dtype)

    def kernel(lists_hbm, tiled_hbm, *rest):
        outs, tiled_ref = rest[: len(legs)], rest[len(legs)]
        lists_ref, sems, sem = rest[len(legs) + 1 :]
        loads = [pltpu.make_async_copy(lists_hbm, lists_ref, sem)]
        for i in range(chunks):
            at = pl.ds(i * chunk, chunk)
            loads.append(pltpu.make_async_copy(tiled_hbm.at[at], tiled_ref.at[at], sems.at[i]))
        for load in loads:
            load.start()
        device = lax.axis_index("space")
        directions = [plan.sends(leg, device) for leg in legs]
        for load in loads:
            load.wait()
        for i, direction in enumerate(directions):
            for j in range(cap):
                outs[i][j] = tiled_ref[lists_ref[0, direction, j]]

    return pl.pallas_call(
        kernel,
        out_shape=[shape] * len(legs) + [pltpu.VMEM(tiled.shape, tiled.dtype)],
        in_specs=[HBM, HBM],
        out_specs=[VMEM] * (len(legs) + 1),
        scratch_shapes=[
            pltpu.SMEM(lists.shape, jnp.int32),
            pltpu.SemaphoreType.DMA((chunks,)),
            pltpu.SemaphoreType.DMA(()),
        ],
        compiler_params=pltpu.CompilerParams(vmem_limit_bytes=4 * MIB),
        name="pick",
    )(in_hbm(lists), in_hbm(tiled))


def local_part(columns, tiled, space_tiles, tree, plan):
    own, nodes, species = tiled.shape
    stored = columns.shape[0]
    slots = plan.slots
    blocks = own // LOCAL_BLOCK
    block = LOCAL_BLOCK * nodes

    def kernel(columns_hbm, x_ref, a_hbm, tree_hbm, product_hbm, *rest):
        p_ref, v_ref, quad_ref, meta_ref, forward_ref, a_ref = rest[:6]
        columns_ref, tree_ref, xs_ref, c_sem, a_sem, t_sem, p_sem = rest[6:]
        device = lax.axis_index("space")

        def load(hbm, ref, sems, b):
            at = pl.ds(b * LOCAL_BLOCK, LOCAL_BLOCK)
            return pltpu.make_async_copy(hbm.at[at], ref.at[at], sems.at[b])

        def store(b):
            return load(p_ref, product_hbm, p_sem, b)

        load_columns = pltpu.make_async_copy(columns_hbm, columns_ref, c_sem)
        load_tree = pltpu.make_async_copy(tree_hbm, tree_ref, t_sem)
        load_columns.start()
        load_tree.start()
        for b in range(blocks):
            load(a_hbm, a_ref, a_sem, b).start()

        def clear(i, _):
            v_ref[i] = jnp.zeros((nodes, species), jnp.float32)
            return 0

        lax.fori_loop(0, slots + 1, clear, 0)
        xs_ref[own] = jnp.zeros((nodes, 2 * species), jnp.bfloat16)

        def prepare(b, _):
            at = pl.ds(b * LOCAL_BLOCK, LOCAL_BLOCK)
            xs_ref[at] = side_by_side(x_ref[at].reshape(block, species)).reshape(LOCAL_BLOCK, nodes, 2 * species)
            return 0

        lax.fori_loop(0, blocks, prepare, 0)
        load_columns.wait()
        load_tree.wait()
        forward = tree_forward(tree_ref[...])
        forward_ref[...] = forward

        def rows(b, carry):
            remote, quad = carry
            load(a_hbm, a_ref, a_sem, b).wait()
            parts = []
            for u in range(LOCAL_BLOCK):
                t = b * LOCAL_BLOCK + u
                tiles, last = [], jnp.int32(0)
                for k in range(stored):
                    column = columns_ref[k, t]
                    last = jnp.maximum(last, column)
                    tiles.append(xs_ref[jnp.minimum(column, own)])
                meta_ref[0, remote] = t
                remote = remote + (last >= own).astype(jnp.int32)
                parts.append(quarters(dot(stacked(a_ref[t]), jnp.concatenate(tiles, axis=0), ((1,), (0,)))))
            product = halves(dot(side_by_side(jnp.concatenate(parts, axis=0)), forward, ((1,), (1,))))
            at = pl.ds(b * LOCAL_BLOCK, LOCAL_BLOCK)
            p_ref[at] = product.reshape(LOCAL_BLOCK, nodes, species)
            store(b).start()
            x = x_ref[at].reshape(block, species)
            return remote, quad + (x * product).reshape(-1, 8, species).sum(axis=0)

        remote, quad = lax.fori_loop(0, blocks, rows, (jnp.int32(0), jnp.zeros((8, species), jnp.float32)))
        quad_ref[...] = quad
        last_row = meta_ref[0, jnp.maximum(remote - 1, 0)]
        for u in range(BLOCK):
            meta_ref[0, remote + u] = last_row
        meta_ref[1 + stored, 0] = remote
        backward = tree_backward(tree_ref[...])

        def remote_rows(b, _):
            rows = [meta_ref[0, b * BLOCK + u] for u in range(BLOCK)]
            x = jnp.concatenate([xs_ref[t] for t in rows], axis=0)
            z = side_by_side(halves(dot(x, backward, ((1,), (0,)))))
            for u, t in enumerate(rows):
                i = b * BLOCK + u
                mine = z[u * nodes : (u + 1) * nodes]
                w = halves(dot(stacked(a_ref[t]), jnp.concatenate([mine, mine], axis=0), ((0,), (0,))))
                for k in range(stored):
                    slot = plan.slot(columns_ref[k, t], own, device)
                    slot = jnp.where(i < remote, slot, slots)
                    meta_ref[1 + k, i] = slot
                    v_ref[slot] += w[k * nodes : (k + 1) * nodes]
            return 0

        lax.fori_loop(0, (remote + BLOCK - 1) // BLOCK, remote_rows, 0)
        for b in range(blocks):
            store(b).wait()

    return pl.pallas_call(
        kernel,
        out_shape=[
            pltpu.HBM(tiled.shape, jnp.float32),
            pltpu.VMEM(tiled.shape, jnp.float32),
            pltpu.VMEM((slots + 1, nodes, species), jnp.float32),
            pltpu.VMEM((8, species), jnp.float32),
            pltpu.SMEM((stored + 2, own + BLOCK), jnp.int32),
            pltpu.VMEM((2 * species, 2 * species), jnp.bfloat16),
            pltpu.VMEM(space_tiles.shape, jnp.float32),
        ],
        in_specs=[HBM, VMEM, HBM, HBM],
        out_specs=[HBM, VMEM, VMEM, VMEM, SMEM, VMEM, VMEM],
        scratch_shapes=[
            pltpu.SMEM(columns.shape, jnp.int32),
            pltpu.VMEM(tree.shape, jnp.float32),
            pltpu.VMEM((own + 1, nodes, 2 * species), jnp.bfloat16),
            pltpu.SemaphoreType.DMA(()),
            pltpu.SemaphoreType.DMA((blocks,)),
            pltpu.SemaphoreType.DMA(()),
            pltpu.SemaphoreType.DMA((blocks,)),
        ],
        compiler_params=pltpu.CompilerParams(vmem_limit_bytes=16 * MIB),
        name="local_part",
    )(in_hbm(columns), tiled, in_hbm(space_tiles), in_hbm(tree))


def remote_quad(v, quad, received):
    species = v.shape[2]
    cap = received[0].shape[0]

    def kernel(v_ref, quad_ref, *rest):
        parts, out_ref = rest[:-1], rest[-1]
        total = quad_ref[...]
        for i, part in enumerate(parts):
            for j in range(cap):
                total = total + (v_ref[i * cap + j] * part[j]).reshape(-1, 8, species).sum(axis=0)
        out_ref[...] = total.sum(axis=0, keepdims=True)

    return pl.pallas_call(
        kernel,
        out_shape=pltpu.VMEM((1, species), jnp.float32),
        in_specs=[VMEM] * (2 + len(received)),
        out_specs=VMEM,
        compiler_params=pltpu.CompilerParams(vmem_limit_bytes=8 * MIB),
        name="remote_quad",
    )(v, quad, *received)


def swap_masks(count):
    masks = [1 << bit for bit in range(count.bit_length() - 1)]
    if 1 << len(masks) != count or len(masks) < 3:
        return []
    return [mask | 1 for mask in masks[2:-1] + [masks[1], masks[-1]]] + [1]


def swap_sum(x, count, changed, put):
    masks = swap_masks(count)
    if not masks:
        return lax.psum(x, "space"), jnp.zeros_like(x), put(changed)
    for i, mask in enumerate(masks[:-1]):
        x = x + lax.ppermute(x, "space", [(j, j ^ mask) for j in range(count)])
        if i == 0:
            x, changed = lax.optimization_barrier((x, changed))
        if i == len(masks) - 2:
            x, product = lax.optimization_barrier((x, put(changed)))
    return x, lax.ppermute(x, "space", [(j, j ^ masks[-1]) for j in range(count)]), product


def remote_part(meta, space_tiles, forward, local, received):
    own, nodes, species = local.shape
    stored = meta.shape[0] - 2
    legs, cap = len(received), received[0].shape[0]
    slots = legs * cap

    def kernel(meta_ref, forward_ref, a_ref, p_ref, *rest):
        parts, (o_ref, xs_ref) = rest[:legs], rest[legs:]
        xs_ref[slots] = jnp.zeros((nodes, 2 * species), jnp.bfloat16)
        for i in range(legs):
            x = parts[i][...].reshape(cap * nodes, species)
            xs_ref[i * cap : (i + 1) * cap] = side_by_side(x).reshape(cap, nodes, 2 * species)
        forward = forward_ref[...]

        def work(b, _):
            rows = [meta_ref[0, b * BLOCK + u] for u in range(BLOCK)]
            sums = []
            for u, t in enumerate(rows):
                tiles = [xs_ref[meta_ref[1 + k, b * BLOCK + u]] for k in range(stored)]
                sums.append(quarters(dot(stacked(a_ref[t]), jnp.concatenate(tiles, axis=0), ((1,), (0,)))))
            added = halves(dot(side_by_side(jnp.concatenate(sums, axis=0)), forward, ((1,), (1,))))
            for u, t in enumerate(rows):
                o_ref[b * BLOCK + u] = p_ref[t] + added[u * nodes : (u + 1) * nodes]
            return 0

        lax.fori_loop(0, (meta_ref[1 + stored, 0] + BLOCK - 1) // BLOCK, work, 0)

    return pl.pallas_call(
        kernel,
        out_shape=pltpu.VMEM((own + BLOCK, nodes, species), jnp.float32),
        in_specs=[SMEM] + [VMEM] * (3 + legs),
        out_specs=VMEM,
        scratch_shapes=[pltpu.VMEM((slots + 1, nodes, 2 * species), jnp.bfloat16)],
        compiler_params=pltpu.CompilerParams(vmem_limit_bytes=16 * MIB),
        name="remote_part",
    )(meta, forward, space_tiles, local, *received)


def store(meta, changed, product):
    own = product.shape[0]
    stored = meta.shape[0] - 2

    def kernel(meta_ref, changed_ref, _, product_hbm, sems):
        remote = meta_ref[1 + stored, 0]

        def copy(i):
            return pltpu.make_async_copy(changed_ref.at[i], product_hbm.at[meta_ref[0, i]], sems.at[i])

        def begin(i, _):
            copy(i).start()
            return 0

        def end(i, _):
            copy(i).wait()
            return 0

        lax.fori_loop(0, remote, begin, 0)
        lax.fori_loop(0, remote, end, 0)

    return pl.pallas_call(
        kernel,
        out_shape=pltpu.HBM(product.shape, jnp.float32),
        in_specs=[SMEM, VMEM, HBM],
        out_specs=HBM,
        scratch_shapes=[pltpu.SemaphoreType.DMA((own,))],
        input_output_aliases={2: 0},
        compiler_params=pltpu.CompilerParams(vmem_limit_bytes=8 * MIB),
        name="store",
    )(meta, changed, in_hbm(product))


def finish(x, y, scale):
    def kernel(x_ref, y_ref, quad_ref):
        quad_ref[0] = jnp.sum(x_ref[...] + y_ref[...]) * scale

    return pl.pallas_call(
        kernel,
        out_shape=jax.ShapeDtypeStruct((1,), jnp.float32),
        in_specs=[VMEM, VMEM],
        out_specs=SMEM,
        compiler_params=pltpu.CompilerParams(vmem_limit_bytes=MIB),
        name="finish",
    )(x, y)


def on_device(signal, space_tiles, tree_precision, send_tiles, column_tiles):
    count = lax.axis_size("space")
    tile_rows, tile_nodes = space_tiles.shape[:2]
    species = signal.shape[1]
    plan = Exchange(count, send_tiles.shape[2])
    tiled = signal.reshape(tile_rows, tile_nodes, species)
    *outgoing, tiled = pick(send_tiles, tiled, plan)
    received = [lax.ppermute(o, "space", plan.route(leg)) for o, leg in zip(outgoing, plan.legs)]
    product, local, v, quad, meta, forward, space_tiles = local_part(
        column_tiles.T, tiled, space_tiles, tree_precision, plan
    )
    share = remote_quad(v, quad, received)
    changed = remote_part(meta, space_tiles, forward, local, received)
    x, y, product = swap_sum(share, count, changed, lambda rows: store(meta, rows, product))
    scale = 1.0 / math.sqrt(count * tile_rows * tile_nodes * species)
    return product.reshape(signal.shape), finish(x, y, scale)


def solution(mesh):
    placed = (
        P(("groups", "space"), None),
        P("space", None, None),
        P("groups", None),
        P("space", None, None),
        P("space", None),
    )
    return jax.shard_map(
        on_device,
        mesh=mesh,
        in_specs=placed,
        out_specs=(P(("groups", "space"), None), P("groups")),
        check_vma=False,
    )
```
